32 devices in a mesh: ctx: 16 (over z, y, x), tp: 2 (over core).
Axes of the slice: x: 2, y: 2, z: 4, core: 2. Of those that a mesh axis runs over, the one named last changes fastest.
Arguments:
- tokens: bfloat16 [4096, 1024], P(('ctx', 'tp')), may hold values from -6 to 6
- positions: int32 [4096], P('ctx'), may hold values from 0 to 1999, as said below
- attention_gain: float32 [1024], replicated, may hold values from 0.25 to 1.75
- query_gain: float32 [64], replicated, may hold values from 0.25 to 1.75
- key_gain: float32 [64], replicated, may hold values from 0.25 to 1.75
- feedforward_gain: float32 [1024], replicated, may hold values from 0.25 to 1.75
- query_weight: bfloat16 [1024, 1024], P('ctx', 'tp'), may hold values from -0.1875 to 0.1875
- key_matrix: bfloat16 [1024, 512], P('ctx', 'tp'), may hold values from -0.1875 to 0.1875
- value_matrix: bfloat16 [1024, 512], P('ctx', 'tp'), may hold values from -0.1875 to 0.1875
- output_weight: bfloat16 [1024, 1024], P('ctx', 'tp'), may hold values from -3 to 3
- gate_weight: bfloat16 [1024, 4608], P('ctx', 'tp'), may hold values from -0.1875 to 0.1875
- up_weight: bfloat16 [1024, 4608], P('ctx', 'tp'), may hold values from -0.1875 to 0.1875
- down_weight: bfloat16 [1024, 4608], P('ctx', 'tp'), may hold values from -0.09375 to 0.09375
- cotangent: bfloat16 [4096, 1024], P(('ctx', 'tp')), may hold values from -9 to 9
Outputs:
- block_output: bfloat16 [4096, 1024], P(('ctx', 'tp'))
- dtokens: float32 [4096, 1024], P(('ctx', 'tp'))
- dattention_gain: float32 [1024], replicated
- dquery_gain: float32 [64], replicated
- dkey_gain: float32 [64], replicated
- dfeedforward_gain: float32 [1024], replicated
- dquery_weight: float32 [1024, 1024], P('ctx', 'tp')
- dkey_weight: float32 [1024, 512], P('ctx', 'tp')
- dvalue_weight: float32 [1024, 512], P('ctx', 'tp')
- doutput_weight: float32 [1024, 1024], P('ctx', 'tp')
- dgate_weight: float32 [1024, 4608], P('ctx', 'tp')
- dup_weight: float32 [1024, 4608], P('ctx', 'tp')
- ddown_weight: float32 [1024, 4608], P('ctx', 'tp')
The draws below stay inside these ranges and needn't reach their ends.
Inputs may be any that keep to these rules, and one draw needn't show every extreme that they name: `positions`: documents are runs of consecutive tokens; position 0 starts one, and each following token of it counts one up. A document has 200 to 2000 tokens, except the last one, which the stream's end may cut; one has exactly 2000.
All inputs are finite; a program needn't handle non-finite values.
Results may differ from the reference program's by a relative error of at most 0.018.
Values may be sent and summed in bfloat16 or wider, within the bound.
No kernel may reach another device: no remote copies, remote signals or barrier semaphores. Data moves between devices by JAX's collectives and lax.ppermute only.
A program may use at most 128 MiB of HBM per device.

```python
import math
import jax
import jax.numpy as jnp
from jax import lax

MODEL_WIDTH = 1024
QUERY_HEADS = 16
KEY_VALUE_HEADS = 8
HEAD_SIZE = 64
FF = 4608
DOC_MOST = 2000
DOC_LEAST = 200
STREAM_TOKENS = 4096


def draw_positions(key, part):
    document_count = STREAM_TOKENS // DOC_LEAST + 1
    lengths = jax.random.randint(jax.random.fold_in(key, 11), (document_count,), DOC_LEAST, DOC_MOST + 1)
    longest_slot = jax.random.randint(jax.random.fold_in(key, 12), (), 0, max(STREAM_TOKENS // DOC_MOST - 1, 1))
    lengths = jnp.where(jnp.arange(document_count) == longest_slot, DOC_MOST, lengths)
    document_ends = jnp.cumsum(lengths)
    starts = document_ends - lengths
    token_index = jnp.arange(STREAM_TOKENS, dtype=jnp.int32)
    document = jnp.searchsorted(document_ends, token_index, side='right')
    return (token_index - jnp.take(starts, document)).astype(jnp.int32)


def draw_cotangent(key, part):
    rising = 0.6 * jnp.exp(jnp.log(3.0) * jnp.arange(STREAM_TOKENS, dtype=jnp.float32) / STREAM_TOKENS)[:, None]
    noise = jnp.clip(jax.random.normal(key, (STREAM_TOKENS, MODEL_WIDTH), jnp.float32), -5.0, 5.0)
    return (noise * rising).astype(jnp.bfloat16)


def shard_levels(rng, extent, cuts, low, high):
    def one(dim, shards_of):
        steps = jax.random.uniform(jax.random.fold_in(jax.random.fold_in(rng, 6), dim), (shards_of,), jnp.float32, low / len(cuts), high / len(cuts))
        return jnp.repeat(jnp.exp(steps), extent[dim] // shards_of).reshape((-1,) + (1,) * (len(extent) - dim - 1))

    gain = one(*cuts[0])
    for cut in cuts[1:]:
        gain = gain * one(*cut)
    return gain


def gaussian(rng, shape, width, limit, pieces=(), kind=jnp.bfloat16):
    gain = shard_levels(rng, shape, pieces, -0.22, 0.18) if pieces else 1.0
    result = jax.random.normal(rng, shape, jnp.float32) * width * gain
    return jnp.minimum(jnp.maximum(result, -limit), limit).astype(kind)


def setup_inputs(seed: int = 0) -> dict:
    key_of = jax.random.split(jax.random.key(seed), 15)
    return {
        "tokens": gaussian(key_of[0], (STREAM_TOKENS, MODEL_WIDTH), 1.0, 6.0, ((0, 32),)),
        "positions": draw_positions(jax.random.fold_in(key_of[14], 71), 0),
        "attention_gain": jnp.clip(1.0 + 0.15 * jax.random.normal(key_of[2], (MODEL_WIDTH,), jnp.float32), 0.25, 1.75),
        "query_gain": jnp.clip(1.0 + 0.15 * jax.random.normal(key_of[3], (HEAD_SIZE,), jnp.float32), 0.25, 1.75),
        "key_gain": jnp.clip(1.0 + 0.15 * jax.random.normal(key_of[4], (HEAD_SIZE,), jnp.float32), 0.25, 1.75),
        "feedforward_gain": jnp.clip(1.0 + 0.15 * jax.random.normal(key_of[5], (MODEL_WIDTH,), jnp.float32), 0.25, 1.75),
        "query_weight": gaussian(key_of[6], (MODEL_WIDTH, QUERY_HEADS * HEAD_SIZE), MODEL_WIDTH ** -0.5, 0.1875, ((0, 16), (1, 2))),
        "key_matrix": gaussian(key_of[7], (MODEL_WIDTH, KEY_VALUE_HEADS * HEAD_SIZE), MODEL_WIDTH ** -0.5, 0.1875, ((0, 16), (1, 2))),
        "value_matrix": gaussian(key_of[8], (MODEL_WIDTH, KEY_VALUE_HEADS * HEAD_SIZE), MODEL_WIDTH ** -0.5, 0.1875, ((0, 16), (1, 2))),
        "output_weight": gaussian(key_of[9], (MODEL_WIDTH, QUERY_HEADS * HEAD_SIZE), (max(QUERY_HEADS * HEAD_SIZE // 256, 1)) ** -0.5, 3.0, ((0, 16), (1, 2))),
        "gate_weight": gaussian(key_of[10], (MODEL_WIDTH, FF), MODEL_WIDTH ** -0.5, 0.1875, ((0, 16), (1, 2))),
        "up_weight": gaussian(key_of[11], (MODEL_WIDTH, FF), MODEL_WIDTH ** -0.5, 0.1875, ((0, 16), (1, 2))),
        "down_weight": gaussian(key_of[12], (MODEL_WIDTH, FF), FF ** -0.5, 0.09375, ((0, 16), (1, 2))),
        "cotangent": draw_cotangent(jax.random.fold_in(key_of[14], 71), 0),
    }


epsilon = 1e-05
rope_base = 1000000.0
masked_value = -1e+30
peak_value = lax.Precision.HIGHEST

@jax.custom_vjp
def low(v):
    return lax.optimization_barrier(v.astype(jnp.bfloat16)).astype(jnp.float32)

@jax.custom_vjp
def low_back(v):
    return v

def low_keep(v):
    return (low(v), None)

def low_pass(kept, grad):
    return (grad,)

def back_keep(v):
    return (v, None)

def back_low(kept, grad):
    return (low(grad),)
low.defvjp(low_keep, low_pass)
low_back.defvjp(back_keep, back_low)

def normalize(values, gain_vector):
    return values * lax.rsqrt(lax.optimization_barrier(jnp.mean(values * values, axis=-1, keepdims=True)) + epsilon) * gain_vector

def rope_tables(positions):
    half_width = HEAD_SIZE // 2
    frequency = rope_base ** (-2.0 * jnp.arange(half_width, dtype=jnp.float32) / HEAD_SIZE)
    angles = positions.astype(jnp.float32)[:, None] * frequency[None, :]
    return (jnp.cos(angles)[:, None, :], jnp.sin(angles)[:, None, :])

def rotate(values, cosine_table, sine_table):
    half_width = HEAD_SIZE // 2
    first_half = values[..., :half_width]
    second = values[..., half_width:]
    return jnp.concatenate([first_half * cosine_table - second * sine_table, second * cosine_table + first_half * sine_table], axis=-1)

def attend(query_matrix_rows, keys, value_lines, positions):
    group_width = QUERY_HEADS // KEY_VALUE_HEADS
    block_rows = math.gcd(STREAM_TOKENS, 512)
    sliding_span = (DOC_MOST + block_rows - 2) // block_rows * block_rows
    block_count = STREAM_TOKENS // block_rows
    query_matrix_rows = query_matrix_rows.reshape(STREAM_TOKENS, KEY_VALUE_HEADS, group_width, HEAD_SIZE)
    pad_amount = jnp.zeros((sliding_span, KEY_VALUE_HEADS, HEAD_SIZE), jnp.float32)
    key_padded = jnp.concatenate([pad_amount, keys], axis=0)
    value_padded = jnp.concatenate([pad_amount, value_lines], axis=0)
    offsets = jnp.arange(sliding_span + block_rows, dtype=jnp.int32)[None, :] - sliding_span - jnp.arange(block_rows, dtype=jnp.int32)[:, None]

    def one_block(block_index):
        start_row = (block_index * block_rows).astype(jnp.int32)
        query_block = lax.dynamic_slice_in_dim(query_matrix_rows, start_row, block_rows, 0)
        key_block = lax.dynamic_slice_in_dim(key_padded, start_row, sliding_span + block_rows, 0)
        value_block = lax.dynamic_slice_in_dim(value_padded, start_row, sliding_span + block_rows, 0)
        position_block = lax.dynamic_slice_in_dim(positions, start_row, block_rows, 0)
        scores = jnp.einsum('qkgd,tkd->kgqt', query_block, key_block, precision=peak_value) * HEAD_SIZE ** (-0.5)
        scores = low_back(scores)
        visible = (offsets <= 0) & (offsets >= -position_block[:, None])
        scores = jnp.where(visible, scores, masked_value)
        largest = lax.optimization_barrier(jnp.max(scores, axis=-1, keepdims=True))
        exponent = jnp.exp(scores - largest)
        probabilities = low(exponent / lax.optimization_barrier(jnp.sum(exponent, axis=-1, keepdims=True)))
        return jnp.einsum('kgqt,tkd->qkgd', probabilities, value_block, precision=peak_value)
    results = lax.map(jax.checkpoint(one_block), jnp.arange(block_count, dtype=jnp.int32))
    return results.reshape(STREAM_TOKENS, QUERY_HEADS * HEAD_SIZE)

def forward(tokens, attention_gain, query_gain, key_gain, feedforward_gain, query_weight, key_matrix, value_matrix, output_weight, gate_weight, up_weight, down_weight, positions):
    cosine_table, sine_table = rope_tables(positions)
    attention_entry = low(normalize(tokens, attention_gain))
    query_pre = low_back(jnp.dot(attention_entry, query_weight, precision=peak_value, preferred_element_type=jnp.float32)).reshape(STREAM_TOKENS, QUERY_HEADS, HEAD_SIZE)
    key_before_rotary = low_back(jnp.dot(attention_entry, key_matrix, precision=peak_value, preferred_element_type=jnp.float32)).reshape(STREAM_TOKENS, KEY_VALUE_HEADS, HEAD_SIZE)
    value_lines = low(low_back(jnp.dot(attention_entry, value_matrix, precision=peak_value, preferred_element_type=jnp.float32))).reshape(STREAM_TOKENS, KEY_VALUE_HEADS, HEAD_SIZE)
    query_matrix_rows = low(rotate(normalize(query_pre, query_gain), cosine_table, sine_table))
    keys = low(rotate(normalize(key_before_rotary, key_gain), cosine_table, sine_table))
    attended = low(low_back(attend(query_matrix_rows, keys, value_lines, positions)))
    hidden = tokens + low_back(jnp.dot(attended, output_weight.T, precision=peak_value, preferred_element_type=jnp.float32))
    feed_input = low(normalize(hidden, feedforward_gain))
    gate_values = low_back(jnp.dot(feed_input, gate_weight, precision=peak_value, preferred_element_type=jnp.float32))
    up_values = low_back(jnp.dot(feed_input, up_weight, precision=peak_value, preferred_element_type=jnp.float32))
    activation = low(jax.nn.silu(gate_values) * up_values)
    return hidden + low_back(jnp.dot(activation, down_weight.T, precision=peak_value, preferred_element_type=jnp.float32))

def reference(tokens, positions, attention_gain, query_gain, key_gain, feedforward_gain, query_weight, key_matrix, value_matrix, output_weight, gate_weight, up_weight, down_weight, cotangent):

    def whole_block(*arrays):
        return forward(*arrays, positions)
    primals = (tokens.astype(jnp.float32), attention_gain, query_gain, key_gain, feedforward_gain, query_weight.astype(jnp.float32), key_matrix.astype(jnp.float32), value_matrix.astype(jnp.float32), output_weight.astype(jnp.float32), gate_weight.astype(jnp.float32), up_weight.astype(jnp.float32), down_weight.astype(jnp.float32))
    output, pullback = jax.vjp(whole_block, *primals)
    gradients = pullback(cotangent.astype(jnp.float32))
    return (output.astype(jnp.bfloat16), gradients[0], gradients[1], gradients[2], gradients[3], gradients[4], gradients[5], gradients[6], gradients[7], gradients[8], gradients[9], gradients[10], gradients[11])
```

```python
import functools

import jax
import jax.numpy as jnp
from jax import lax
from jax.experimental import pallas as pl
from jax.experimental.pallas import tpu as pltpu
from jax.sharding import PartitionSpec as P

HEAD_SIZE = 64
DOC_MOST = 2000
GROUP = 4
BLOCK = 256

epsilon = 1e-05
rope_base = 1000000.0
score_scale = HEAD_SIZE ** (-0.5)

bf16 = jnp.bfloat16
f32 = jnp.float32


def rms_scale(values):
    return lax.rsqrt(jnp.mean(values * values, axis=-1, keepdims=True) + epsilon)


def norm_back(upstream, values, gain_vector):
    scaling = rms_scale(values)
    normed = values * scaling
    weighted = upstream * gain_vector
    inner_sum = jnp.mean(weighted * normed, axis=-1, keepdims=True)
    return scaling * (weighted - normed * inner_sum)


def swap_core(block):
    return lax.ppermute(block, "tp", [(0, 1), (1, 0)])


def to_member(block, flip):
    size = lax.axis_size("ctx")
    return lax.ppermute(block, "ctx", [(i, i ^ flip) for i in range(size)])


def to_later(block, by):
    size = lax.axis_size("ctx")
    return lax.ppermute(block, "ctx", [(i, i + by) for i in range(size) if 0 <= i + by < size])


def gather_rows(rows):
    own = jnp.concatenate([rows] + [to_member(rows, flip) for flip in range(1, GROUP)], axis=0)
    return jnp.concatenate([own, swap_core(own)], axis=0)


def scatter_rows(partial):
    half = partial.shape[0] // 2
    mine = partial[:half] + swap_core(partial[half:].astype(bf16)).astype(f32)
    count = half // GROUP
    total = mine[:count]
    for flip in range(1, GROUP):
        part = mine[flip * count : (flip + 1) * count].astype(bf16)
        total = total + to_member(part, flip).astype(f32)
    return total


VMEM_WHOLE = pl.BlockSpec(memory_space=pltpu.VMEM)
SMEM_WHOLE = pl.BlockSpec(memory_space=pltpu.SMEM)


def call(kernel, outs, in_specs, scratch=(), name=None):
    return pl.pallas_call(
        kernel,
        out_shape=[jax.ShapeDtypeStruct(s, d) for s, d in outs],
        in_specs=in_specs,
        out_specs=[VMEM_WHOLE] * len(outs),
        scratch_shapes=list(scratch),
        name=name,
    )


def lanes(shape):
    return lax.broadcasted_iota(jnp.int32, shape, len(shape) - 1)


def head_mean(values, ones):
    high = values.astype(bf16)
    low = (values - high.astype(f32)).astype(bf16)
    return jnp.dot(high, ones, preferred_element_type=f32) + jnp.dot(
        low, ones, preferred_element_type=f32
    )


def block_ones():
    row = lax.broadcasted_iota(jnp.int32, (128, 128), 0) // HEAD_SIZE
    col = lax.broadcasted_iota(jnp.int32, (128, 128), 1) // HEAD_SIZE
    return jnp.where(row == col, 1.0 / HEAD_SIZE, 0.0).astype(bf16)


def swap_halves(values):
    lane = lanes(values.shape)
    return jnp.where(
        lane % HEAD_SIZE < HEAD_SIZE // 2,
        pltpu.roll(values, 128 - HEAD_SIZE // 2, 1),
        pltpu.roll(values, HEAD_SIZE // 2, 1),
    )


def rotary_kernel(order, pre_ref, cos_ref, sin_ref, qg_ref, kg_ref, q_ref, kv_ref):
    ones = block_ones()
    rows = 128

    def step(j, carry):
        here = pl.ds(pl.multiple_of(j * rows, rows), rows)
        there = pl.ds(pl.multiple_of(order[j] * rows, rows), rows)
        cosine, sine = cos_ref[here, :], sin_ref[here, :]
        lane = lanes((rows, 128))
        first = lane < HEAD_SIZE

        def turned(raw, gain):
            normed = raw * lax.rsqrt(head_mean(raw * raw, ones) + epsilon) * gain
            return normed * cosine + swap_halves(normed) * sine

        query = turned(pre_ref[there, 0:128], qg_ref[...])
        q_ref[0, here, :] = jnp.where(first, query, 0.0).astype(bf16)
        q_ref[1, here, :] = jnp.where(first, pltpu.roll(query, HEAD_SIZE, 1), 0.0).astype(bf16)
        raw = pre_ref[there, 128:256]
        kv_ref[here, :] = jnp.where(first, turned(raw, kg_ref[...]), raw).astype(bf16)
        return carry

    lax.fori_loop(0, pre_ref.shape[0] // rows, step, 0)


def both_heads(ref, here):
    return jnp.concatenate([ref[0, here, :], ref[1, here, :]], axis=0)


def dot_t(a, b):
    return lax.dot_general(a, b, (((1,), (1,)), ((), ())), preferred_element_type=f32)


def dot_rows(a, b):
    return lax.dot_general(a, b, (((0,), (0,)), ((), ())), preferred_element_type=f32)


def wide(tile):
    tall = jnp.concatenate([tile, tile], axis=0)
    return jnp.concatenate([tall, tall], axis=1)


def wide_lanes(tile):
    return jnp.concatenate([tile, tile], axis=1)


def seen(start_tile, base, query_base, causal):
    key = lanes((2 * BLOCK, BLOCK)) + base
    visible = key >= wide(start_tile)
    if causal:
        row = lax.broadcasted_iota(jnp.int32, (2 * BLOCK, BLOCK), 0)
        visible = visible & (key <= (row % BLOCK) + query_base)
    return visible


def attend_block(query, kv, visible):
    scores = dot_t(query, kv) * score_scale
    weights = jnp.where(visible, jnp.exp(scores), 0.0).astype(bf16)
    one_value = jnp.where(lanes(kv.shape) < HEAD_SIZE, 1.0, kv.astype(f32)).astype(bf16)
    return jnp.dot(weights, one_value, preferred_element_type=f32)


def attend_own_kernel(low, start_ref, q_ref, kv_ref, o_ref, acc):
    for i in range(q_ref.shape[1] // BLOCK):
        here = pl.ds(i * BLOCK, BLOCK)
        query = both_heads(q_ref, here)
        start = start_ref[here, :]
        acc[...] = jnp.zeros_like(acc)
        for j in range(i + 1):

            @pl.when(low[i] < (j + 1) * BLOCK)
            def _():
                visible = seen(start, j * BLOCK, i * BLOCK, j == i)
                acc[...] += attend_block(query, kv_ref[pl.ds(j * BLOCK, BLOCK), :], visible)

        o_ref[0, here, :] = acc[0:BLOCK, :]
        o_ref[1, here, :] = acc[BLOCK : 2 * BLOCK, :]


def first_block(low_value, span):
    return jnp.clip((low_value + span) // BLOCK, 0, span // BLOCK)


def attend_halo_kernel(
    low, order, start_ref, q_ref, own_ref, *rest
):
    halo = rest[:-5]
    att_ref, attf_ref, lse_ref, kvs, acc = rest[-5:]
    count = q_ref.shape[1]
    span = count * len(halo)
    for n, ref in enumerate(halo):
        kvs[pl.ds(n * count, count), :] = ref[...]
    for i in range(count // BLOCK):
        here = pl.ds(i * BLOCK, BLOCK)
        query = both_heads(q_ref, here)
        start = start_ref[here, :]
        acc[...] = both_heads(own_ref, here)

        def step(j, carry):
            base = pl.multiple_of(j * BLOCK, BLOCK)
            visible = seen(start, base - span, 0, False)
            acc[...] += attend_block(query, kvs[pl.ds(base, BLOCK), :], visible)
            return carry

        lax.fori_loop(first_block(low[i], span), span // BLOCK, step, 0)
        total = acc[...]
        lane = lanes(total.shape)
        turned = pltpu.roll(total, HEAD_SIZE, 1)
        sums = jnp.where(lane < HEAD_SIZE, total, turned)
        lse = jnp.log(sums)
        lse_ref[0, here, :] = lse[0:BLOCK]
        lse_ref[1, here, :] = lse[BLOCK : 2 * BLOCK]
        value = total / sums
        joined = jnp.where(
            lanes((BLOCK, 128)) < HEAD_SIZE,
            pltpu.roll(value[0:BLOCK], HEAD_SIZE, 1),
            value[BLOCK : 2 * BLOCK],
        )
        attf_ref[here, :] = joined
        for part in range(BLOCK // 128):
            there = pl.ds(pl.multiple_of(order[i * (BLOCK // 128) + part] * 128, 128), 128)
            att_ref[there, :] = joined[part * 128 : (part + 1) * 128].astype(bf16)


def back_block(query, back, kv, lse, delta, visible):
    scores = dot_t(query, kv) * score_scale - lse
    probs = jnp.where(visible, jnp.exp(scores), 0.0)
    back_probs = dot_t(back, kv)
    back_scores = (probs * (back_probs - delta)).astype(bf16)
    back_query = jnp.dot(back_scores, kv, preferred_element_type=f32)
    back_kv = dot_rows(back_scores, query) + dot_rows(probs.astype(bf16), back)
    return back_query, back_kv


def kv_scale(shape):
    return jnp.where(lanes(shape) < HEAD_SIZE, score_scale, 1.0)


def back_halo_kernel(low, order, start_ref, q_ref, do_ref, attf_ref, lse_ref, *rest):
    halo = rest[: (len(rest) - 5) // 2]
    outs = rest[len(halo) : 2 * len(halo)]
    dq_ref, do2_ref, delta_ref, kvs, dkvs = rest[2 * len(halo) :]
    count = q_ref.shape[1]
    span = count * len(halo)
    for n, ref in enumerate(halo):
        kvs[pl.ds(n * count, count), :] = ref[...]
    dkvs[...] = jnp.zeros_like(dkvs)
    dq_ref[...] = jnp.zeros_like(dq_ref)
    for i in range(count // BLOCK):
        here = pl.ds(i * BLOCK, BLOCK)
        parts = []
        for part in range(BLOCK // 128):
            there = pl.ds(pl.multiple_of(order[i * (BLOCK // 128) + part] * 128, 128), 128)
            parts.append(do_ref[there, :].astype(f32))
        back = jnp.concatenate(parts, axis=0)
        first = lanes((BLOCK, 128)) < HEAD_SIZE
        product = back * attf_ref[here, :]
        delta0 = jnp.sum(jnp.where(first, product, 0.0), axis=1, keepdims=True)
        delta1 = jnp.sum(jnp.where(first, 0.0, product), axis=1, keepdims=True)
        delta = jnp.broadcast_to(jnp.concatenate([delta0, delta1], axis=0), (2 * BLOCK, 128))
        delta_ref[0, here, :] = delta[0:BLOCK]
        delta_ref[1, here, :] = delta[BLOCK : 2 * BLOCK]
        back0 = jnp.where(first, 0.0, pltpu.roll(back, HEAD_SIZE, 1)).astype(bf16)
        back1 = jnp.where(first, 0.0, back).astype(bf16)
        do2_ref[0, here, :] = back0
        do2_ref[1, here, :] = back1
        both = jnp.concatenate([back0, back1], axis=0)
        query = both_heads(q_ref, here)
        start = start_ref[here, :]
        lse = wide_lanes(both_heads(lse_ref, here))
        delta = wide_lanes(delta)

        def step(j, carry):
            base = pl.multiple_of(j * BLOCK, BLOCK)
            visible = seen(start, base - span, 0, False)
            back_query, back_kv = back_block(
                query, both, kvs[pl.ds(base, BLOCK), :], lse, delta, visible
            )
            dq_ref[0, here, :] += back_query[0:BLOCK]
            dq_ref[1, here, :] += back_query[BLOCK : 2 * BLOCK]
            dkvs[pl.ds(base, BLOCK), :] += back_kv
            return carry

        lax.fori_loop(first_block(low[i], span), span // BLOCK, step, 0)
    for n, ref in enumerate(outs):
        total = dkvs[pl.ds(n * count, count), :]
        ref[...] = (total * kv_scale(total.shape)).astype(bf16)


def back_own_kernel(
    low, start_ref, q_ref, kv_ref, do2_ref, delta_ref, lse_ref, dq_in_ref, dq_ref, dkv_ref
):
    count = q_ref.shape[1]
    dkv_ref[...] = jnp.zeros_like(dkv_ref)
    dq_ref[...] = dq_in_ref[...]
    for i in range(count // BLOCK):
        here = pl.ds(i * BLOCK, BLOCK)
        query = both_heads(q_ref, here)
        back = both_heads(do2_ref, here)
        start = start_ref[here, :]
        lse = wide_lanes(both_heads(lse_ref, here))
        delta = wide_lanes(both_heads(delta_ref, here))
        for j in range(i + 1):

            @pl.when(low[i] < (j + 1) * BLOCK)
            def _():
                visible = seen(start, j * BLOCK, i * BLOCK, j == i)
                keys = pl.ds(j * BLOCK, BLOCK)
                back_query, back_kv = back_block(
                    query, back, kv_ref[keys, :], lse, delta, visible
                )
                dq_ref[0, here, :] += back_query[0:BLOCK]
                dq_ref[1, here, :] += back_query[BLOCK : 2 * BLOCK]
                dkv_ref[keys, :] += back_kv

    total = dkv_ref[...]
    dkv_ref[...] = total * kv_scale(total.shape)


def rotary_back_kernel(
    order, pre_ref, cos_ref, sin_ref, qg_ref, kg_ref, dq_ref, dkv_ref, *rest
):
    received = rest[:-2]
    out_ref, gain_ref = rest[-2:]
    ones = block_ones()
    rows = 128
    gain_ref[...] = jnp.zeros_like(gain_ref)

    def step(j, carry):
        here = pl.ds(pl.multiple_of(j * rows, rows), rows)
        there = pl.ds(pl.multiple_of(order[j] * rows, rows), rows)
        cosine, sine = cos_ref[here, :], sin_ref[here, :]
        first = lanes((rows, 128)) < HEAD_SIZE

        def back(upstream, raw, gain):
            turned = upstream * cosine - swap_halves(upstream) * sine
            scaling = lax.rsqrt(head_mean(raw * raw, ones) + epsilon)
            normed = raw * scaling
            weighted = turned * gain
            inner = head_mean(weighted * normed, ones)
            return scaling * (weighted - normed * inner), turned * normed

        upstream = (
            jnp.where(first, dq_ref[0, here, :], pltpu.roll(dq_ref[1, here, :], HEAD_SIZE, 1))
            * score_scale
        )
        back_query, rows_query = back(upstream, pre_ref[there, 0:128], qg_ref[...])
        out_ref[there, 0:128] = back_query.astype(bf16)
        upstream = dkv_ref[here, :]
        for ref in received:
            upstream = upstream + ref[here, :].astype(f32)
        back_key, rows_key = back(upstream, pre_ref[there, 128:256], kg_ref[...])
        out_ref[there, 128:256] = jnp.where(first, back_key, upstream).astype(bf16)
        gain_ref[0:1, :] += jnp.sum(rows_query, axis=0, keepdims=True)
        gain_ref[1:2, :] += jnp.sum(jnp.where(first, rows_key, 0.0), axis=0, keepdims=True)
        return carry

    lax.fori_loop(0, pre_ref.shape[0] // rows, step, 0)


def on_device(
    tokens,
    positions,
    attention_gain,
    query_gain,
    key_gain,
    feedforward_gain,
    query_weight,
    key_matrix,
    value_matrix,
    output_weight,
    gate_weight,
    up_weight,
    down_weight,
    cotangent,
):
    size = lax.axis_size("ctx")
    outer = size // GROUP
    groups = [[GROUP * z + m for m in range(GROUP)] for z in range(outer)]
    columns = [[GROUP * z + m for z in range(outer)] for m in range(GROUP)]
    shard_rows, width = query_weight.shape[0], tokens.shape[1]
    own_rows = tokens.shape[0]
    count = 2 * GROUP * own_rows
    halo_groups = -(-(DOC_MOST - 1) // count)
    member = lax.axis_index("ctx") % GROUP
    core = lax.axis_index("tp")

    def split(weight):
        return weight.reshape(shard_rows, GROUP, -1)

    attention_pack = jnp.concatenate(
        [split(query_weight), split(key_matrix), split(value_matrix), split(output_weight)], axis=2
    ).transpose(1, 0, 2)
    attention_weights = lax.all_to_all(
        jnp.tile(attention_pack, (outer, 1, 1)), "ctx", 0, 0, tiled=True
    ).reshape(width, -1)
    qkv_weight = attention_weights[:, :256]
    out_weight = attention_weights[:, 256:]

    def columns_of(weight):
        pack = split(weight).transpose(1, 0, 2)
        rows = lax.all_to_all(pack, "ctx", 0, 0, axis_index_groups=groups, tiled=True)
        rows = rows.reshape(GROUP * shard_rows, -1)
        return lax.all_gather(rows, "ctx", axis=0, axis_index_groups=columns, tiled=True)

    gate_full = columns_of(gate_weight)
    up_full = columns_of(up_weight)
    down_full = columns_of(down_weight)

    residual = tokens.astype(f32)
    normed_rows = (residual * rms_scale(residual) * attention_gain).astype(bf16)
    attention_entry = gather_rows(normed_rows)
    cotangent_rows = gather_rows(cotangent)

    block = jnp.arange(2 * GROUP, dtype=jnp.int32)
    order = ((block % 2) ^ core) * GROUP + ((block // 2) ^ member)
    place = positions.reshape(2, own_rows)
    near = jnp.stack([place] + [to_member(place, flip) for flip in range(1, GROUP)])
    near = near[jnp.arange(GROUP, dtype=jnp.int32) ^ member].reshape(count)
    start = jnp.arange(count, dtype=jnp.int32) - near
    low = start[::BLOCK]
    start_tile = jnp.broadcast_to(start[:, None], (count, 128))
    frequency = rope_base ** (
        -2.0 * jnp.arange(HEAD_SIZE // 2, dtype=f32) / HEAD_SIZE
    )
    angles = near.astype(f32)[:, None] * jnp.tile(frequency, 4)[None, :]
    cosine = jnp.cos(angles)
    sign = jnp.where(jnp.arange(128) % HEAD_SIZE < HEAD_SIZE // 2, -1.0, 1.0)
    sine = jnp.sin(angles) * sign[None, :]
    query_gains = jnp.tile(query_gain, 2)[None, :]
    key_gains = jnp.tile(key_gain, 2)[None, :]

    pre = jnp.dot(attention_entry, qkv_weight, preferred_element_type=f32)
    query, kv = call(
        rotary_kernel,
        [((2, count, 128), bf16), ((count, 128), bf16)],
        [SMEM_WHOLE] + [VMEM_WHOLE] * 5,
        name="rotary",
    )(order, pre, cosine, sine, query_gains, key_gains)
    halo = [to_later(kv, GROUP * n) for n in range(halo_groups, 0, -1)]
    (own_part,) = call(
        attend_own_kernel,
        [((2, count, 128), f32)],
        [SMEM_WHOLE] + [VMEM_WHOLE] * 3,
        [pltpu.VMEM((2 * BLOCK, 128), f32)],
        name="attend_own",
    )(low, start_tile, query, kv)
    attended, attended_wide, lse = call(
        attend_halo_kernel,
        [((count, 128), bf16), ((count, 128), f32), ((2, count, 128), f32)],
        [SMEM_WHOLE] * 2 + [VMEM_WHOLE] * (3 + halo_groups),
        [pltpu.VMEM((halo_groups * count, 128), bf16), pltpu.VMEM((2 * BLOCK, 128), f32)],
        name="attend_halo",
    )(low, order, start_tile, query, own_part, *halo)
    attention_part = dot_t(attended, out_weight)
    hidden = residual + scatter_rows(attention_part)

    feed_rows = (hidden * rms_scale(hidden) * feedforward_gain).astype(bf16)
    feed_input = gather_rows(feed_rows)
    back_activation = jnp.dot(cotangent_rows, down_full, preferred_element_type=f32)
    gate_values = jnp.dot(feed_input, gate_full, preferred_element_type=f32)
    up_values = jnp.dot(feed_input, up_full, preferred_element_type=f32)
    sigmoid_gate = jax.nn.sigmoid(gate_values)
    silu_gate = gate_values * sigmoid_gate
    activation = (silu_gate * up_values).astype(bf16)
    back_gate = (
        back_activation * up_values * sigmoid_gate * (1.0 + gate_values * (1.0 - sigmoid_gate))
    ).astype(bf16)
    back_up = (back_activation * silu_gate).astype(bf16)
    back_feed = dot_t(back_gate, gate_full) + dot_t(back_up, up_full)
    back_feed_rows = scatter_rows(back_feed)
    gate_slope = dot_rows(feed_input, back_gate)
    up_slope = dot_rows(feed_input, back_up)
    down_slope = dot_rows(cotangent_rows, activation)
    block_output = (hidden + scatter_rows(dot_t(activation, down_full))).astype(bf16)

    def rows_of(slope):
        part = lax.psum_scatter(
            slope.astype(bf16), "ctx", scatter_dimension=0, axis_index_groups=columns, tiled=True
        )
        part = part.reshape(GROUP, shard_rows, -1)
        part = lax.all_to_all(part, "ctx", 0, 0, axis_index_groups=groups, tiled=True)
        return part.transpose(1, 0, 2).reshape(shard_rows, -1).astype(f32)

    gate_out, up_out, down_out = rows_of(gate_slope), rows_of(up_slope), rows_of(down_slope)

    back_hidden = cotangent.astype(f32) + norm_back(back_feed_rows, hidden, feedforward_gain)
    residual_rows = gather_rows(back_hidden.astype(bf16))
    back_attended = jnp.dot(residual_rows, out_weight, preferred_element_type=f32).astype(bf16)
    output_slope = dot_rows(residual_rows, attended)
    *back_halo, back_query_part, back_two, delta = call(
        back_halo_kernel,
        [((count, 128), bf16)] * halo_groups
        + [((2, count, 128), f32), ((2, count, 128), bf16), ((2, count, 128), f32)],
        [SMEM_WHOLE] * 2 + [VMEM_WHOLE] * (5 + halo_groups),
        [
            pltpu.VMEM((halo_groups * count, 128), bf16),
            pltpu.VMEM((halo_groups * count, 128), f32),
        ],
        name="back_halo",
    )(low, order, start_tile, query, back_attended, attended_wide, lse, *halo)
    received = [
        to_later(part, -GROUP * n) for part, n in zip(back_halo, range(halo_groups, 0, -1))
    ]
    back_query, back_kv = call(
        back_own_kernel,
        [((2, count, 128), f32), ((count, 128), f32)],
        [SMEM_WHOLE] + [VMEM_WHOLE] * 7,
        name="back_own",
    )(low, start_tile, query, kv, back_two, delta, lse, back_query_part)
    back_pre, head_gains = call(
        rotary_back_kernel,
        [((count, 256), bf16), ((8, 128), f32)],
        [SMEM_WHOLE] + [VMEM_WHOLE] * (7 + halo_groups),
        name="rotary_back",
    )(order, pre, cosine, sine, query_gains, key_gains, back_query, back_kv, *received)

    back_input = dot_t(back_pre, qkv_weight)
    back_input_rows = scatter_rows(back_input)
    dtokens = back_hidden + norm_back(back_input_rows, residual, attention_gain)
    qkv_slope = dot_rows(attention_entry, back_pre)

    attention_gain_part = jnp.sum(back_input_rows * residual * rms_scale(residual), axis=0)
    feed_gain_part = jnp.sum(back_feed_rows * hidden * rms_scale(hidden), axis=0)
    gains = jnp.concatenate(
        [attention_gain_part, feed_gain_part, head_gains[0], head_gains[1]]
    )[None, :]
    everyone = size * lax.axis_size("tp")
    gains = lax.all_to_all(
        jnp.tile(gains, (everyone, 1)), ("ctx", "tp"), 0, 0, tiled=True
    ).sum(axis=0)

    slope = jnp.concatenate([qkv_slope, output_slope], axis=1).astype(bf16)
    slope = lax.all_to_all(slope.reshape(size, shard_rows, -1), "ctx", 0, 0, tiled=True)
    slope = slope.reshape(outer, GROUP, shard_rows, -1).astype(f32).sum(axis=0)
    slope = slope.transpose(1, 0, 2)

    def piece(first, last):
        return slope[:, :, first:last].reshape(shard_rows, -1)

    return (
        block_output,
        dtokens,
        gains[:width],
        gains[2 * width : 2 * width + 64] + gains[2 * width + 64 : 2 * width + 128],
        gains[2 * width + 128 : 2 * width + 192],
        gains[width : 2 * width],
        piece(0, 128),
        piece(128, 192),
        piece(192, 256),
        piece(256, 384),
        gate_out,
        up_out,
        down_out,
    )


def solution(mesh):
    rows = P(("ctx", "tp"), None)
    weight = P("ctx", "tp")
    return jax.shard_map(
        on_device,
        mesh=mesh,
        in_specs=(rows, P("ctx"), P(), P(), P(), P()) + (weight,) * 7 + (rows,),
        out_specs=(rows, rows, P(), P(), P(), P()) + (weight,) * 7,
        check_vma=False,
    )
```

```python
import functools

import jax
import jax.numpy as jnp
from jax import lax
from jax.experimental import pallas as pl
from jax.experimental.pallas import tpu as pltpu
from jax.sharding import PartitionSpec as P

HEAD_SIZE = 64
DOC_MOST = 2000
GROUP = 4
BLOCK = 256

epsilon = 1e-05
rope_base = 1000000.0
score_scale = HEAD_SIZE ** (-0.5)

bf16 = jnp.bfloat16
f32 = jnp.float32


def rms_scale(values):
    return lax.rsqrt(jnp.mean(values * values, axis=-1, keepdims=True) + epsilon)


def norm_back(upstream, values, gain_vector):
    scaling = rms_scale(values)
    normed = values * scaling
    weighted = upstream * gain_vector
    inner_sum = jnp.mean(weighted * normed, axis=-1, keepdims=True)
    return scaling * (weighted - normed * inner_sum)


def swap_core(block):
    return lax.ppermute(block, "tp", [(0, 1), (1, 0)])


def to_member(block, flip):
    size = lax.axis_size("ctx")
    return lax.ppermute(block, "ctx", [(i, i ^ flip) for i in range(size)])


def to_later(block, by):
    size = lax.axis_size("ctx")
    return lax.ppermute(block, "ctx", [(i, i + by) for i in range(size) if 0 <= i + by < size])


VMEM_WHOLE = pl.BlockSpec(memory_space=pltpu.VMEM)
SMEM_WHOLE = pl.BlockSpec(memory_space=pltpu.SMEM)


def call(kernel, outs, in_specs, scratch=(), name=None):
    return pl.pallas_call(
        kernel,
        out_shape=[jax.ShapeDtypeStruct(s, d) for s, d in outs],
        in_specs=in_specs,
        out_specs=[VMEM_WHOLE] * len(outs),
        scratch_shapes=list(scratch),
        name=name,
    )


def lanes(shape):
    return lax.broadcasted_iota(jnp.int32, shape, len(shape) - 1)


def head_mean(values, ones):
    high = values.astype(bf16)
    low = (values - high.astype(f32)).astype(bf16)
    return jnp.dot(high, ones, preferred_element_type=f32) + jnp.dot(
        low, ones, preferred_element_type=f32
    )


def block_ones():
    row = lax.broadcasted_iota(jnp.int32, (128, 128), 0) // HEAD_SIZE
    col = lax.broadcasted_iota(jnp.int32, (128, 128), 1) // HEAD_SIZE
    return jnp.where(row == col, 1.0 / HEAD_SIZE, 0.0).astype(bf16)


def swap_halves(values):
    lane = lanes(values.shape)
    return jnp.where(
        lane % HEAD_SIZE < HEAD_SIZE // 2,
        pltpu.roll(values, 128 - HEAD_SIZE // 2, 1),
        pltpu.roll(values, HEAD_SIZE // 2, 1),
    )


def rotary_kernel(
    order, a_ref, b_ref, w_ref, cos_ref, sin_ref, qg_ref, kg_ref, q_ref, kv_ref, pre_ref
):
    ones = block_ones()
    rows = 128
    half = a_ref.shape[0]
    pre_ref[0:half, :] = jnp.dot(a_ref[...], w_ref[...], preferred_element_type=f32)
    pre_ref[half:, :] = jnp.dot(b_ref[...], w_ref[...], preferred_element_type=f32)

    def step(j, carry):
        here = pl.ds(pl.multiple_of(j * rows, rows), rows)
        there = pl.ds(pl.multiple_of(order[j] * rows, rows), rows)
        cosine, sine = cos_ref[here, :], sin_ref[here, :]
        lane = lanes((rows, 128))
        first = lane < HEAD_SIZE

        def turned(raw, gain):
            normed = raw * lax.rsqrt(head_mean(raw * raw, ones) + epsilon) * gain
            return normed * cosine + swap_halves(normed) * sine

        query = turned(pre_ref[there, 0:128], qg_ref[...])
        q_ref[0, here, :] = jnp.where(first, query, 0.0).astype(bf16)
        q_ref[1, here, :] = jnp.where(first, pltpu.roll(query, HEAD_SIZE, 1), 0.0).astype(bf16)
        raw = pre_ref[there, 128:256]
        kv_ref[here, :] = jnp.where(first, turned(raw, kg_ref[...]), raw).astype(bf16)
        return carry

    lax.fori_loop(0, pre_ref.shape[0] // rows, step, 0, unroll=4)


def both_heads(ref, here):
    return jnp.concatenate([ref[0, here, :], ref[1, here, :]], axis=0)


def dot_t(a, b):
    return lax.dot_general(a, b, (((1,), (1,)), ((), ())), preferred_element_type=f32)


def dot_rows(a, b):
    return lax.dot_general(a, b, (((0,), (0,)), ((), ())), preferred_element_type=f32)


def wide(tile):
    tall = jnp.concatenate([tile, tile], axis=0)
    return jnp.concatenate([tall, tall], axis=1)


def wide_lanes(tile):
    return jnp.concatenate([tile, tile], axis=1)


def seen(start_tile, base, query_base, causal):
    key = lanes((2 * BLOCK, BLOCK)) + base
    visible = key >= wide(start_tile)
    if causal:
        row = lax.broadcasted_iota(jnp.int32, (2 * BLOCK, BLOCK), 0)
        visible = visible & (key <= (row % BLOCK) + query_base)
    return visible


def attend_block(query, kv, visible):
    scores = dot_t(query, kv) * score_scale
    weights = jnp.where(visible, jnp.exp(scores), 0.0).astype(bf16)
    one_value = jnp.where(lanes(kv.shape) < HEAD_SIZE, 1.0, kv.astype(f32)).astype(bf16)
    return jnp.dot(weights, one_value, preferred_element_type=f32)


def attend_own_kernel(low, start_ref, q_ref, kv_ref, o_ref, acc):
    for i in range(q_ref.shape[1] // BLOCK):
        here = pl.ds(i * BLOCK, BLOCK)
        query = both_heads(q_ref, here)
        start = start_ref[here, :]
        acc[...] = jnp.zeros_like(acc)
        for j in range(i + 1):

            @pl.when(low[i] < (j + 1) * BLOCK)
            def _():
                visible = seen(start, j * BLOCK, i * BLOCK, j == i)
                acc[...] += attend_block(query, kv_ref[pl.ds(j * BLOCK, BLOCK), :], visible)

        o_ref[0, here, :] = acc[0:BLOCK, :]
        o_ref[1, here, :] = acc[BLOCK : 2 * BLOCK, :]


def first_block(low_value, span):
    return jnp.clip((low_value + span) // BLOCK, 0, span // BLOCK)


def attend_halo_kernel(
    low, order, start_ref, q_ref, own_ref, *rest
):
    halo = rest[:-5]
    att_ref, attf_ref, lse_ref, kvs, acc = rest[-5:]
    count = q_ref.shape[1]
    span = count * len(halo)
    for n, ref in enumerate(halo):
        kvs[pl.ds(n * count, count), :] = ref[...]
    for i in range(count // BLOCK):
        here = pl.ds(i * BLOCK, BLOCK)
        query = both_heads(q_ref, here)
        start = start_ref[here, :]
        acc[...] = both_heads(own_ref, here)

        def step(j, carry):
            base = pl.multiple_of(j * BLOCK, BLOCK)
            visible = seen(start, base - span, 0, False)
            acc[...] += attend_block(query, kvs[pl.ds(base, BLOCK), :], visible)
            return carry

        lax.fori_loop(first_block(low[i], span), span // BLOCK, step, 0)
        total = acc[...]
        lane = lanes(total.shape)
        turned = pltpu.roll(total, HEAD_SIZE, 1)
        sums = jnp.where(lane < HEAD_SIZE, total, turned)
        lse = jnp.log(sums)
        lse_ref[0, here, :] = lse[0:BLOCK]
        lse_ref[1, here, :] = lse[BLOCK : 2 * BLOCK]
        value = total / sums
        joined = jnp.where(
            lanes((BLOCK, 128)) < HEAD_SIZE,
            pltpu.roll(value[0:BLOCK], HEAD_SIZE, 1),
            value[BLOCK : 2 * BLOCK],
        )
        attf_ref[here, :] = joined
        for part in range(BLOCK // 128):
            there = pl.ds(pl.multiple_of(order[i * (BLOCK // 128) + part] * 128, 128), 128)
            att_ref[there, :] = joined[part * 128 : (part + 1) * 128].astype(bf16)


def back_block(query, back, kv, lse, delta, visible):
    scores = dot_t(query, kv) * score_scale - lse
    probs = jnp.where(visible, jnp.exp(scores), 0.0)
    back_probs = dot_t(back, kv)
    back_scores = (probs * (back_probs - delta)).astype(bf16)
    back_query = jnp.dot(back_scores, kv, preferred_element_type=f32)
    back_kv = dot_rows(back_scores, query) + dot_rows(probs.astype(bf16), back)
    return back_query, back_kv


def kv_scale(shape):
    return jnp.where(lanes(shape) < HEAD_SIZE, score_scale, 1.0)


def back_halo_kernel(
    low, order, start_ref, q_ref, ra_ref, rb_ref, w_ref, attf_ref, lse_ref, *rest
):
    halo = rest[: (len(rest) - 6) // 2]
    outs = rest[len(halo) : 2 * len(halo)]
    dq_ref, do2_ref, delta_ref, kvs, dkvs, do_ref = rest[2 * len(halo) :]
    count = q_ref.shape[1]
    half = ra_ref.shape[0]
    do_ref[0:half, :] = jnp.dot(ra_ref[...], w_ref[...], preferred_element_type=f32)
    do_ref[half:, :] = jnp.dot(rb_ref[...], w_ref[...], preferred_element_type=f32)
    span = count * len(halo)
    for n, ref in enumerate(halo):
        kvs[pl.ds(n * count, count), :] = ref[...]
    dkvs[...] = jnp.zeros_like(dkvs)
    dq_ref[...] = jnp.zeros_like(dq_ref)
    for i in range(count // BLOCK):
        here = pl.ds(i * BLOCK, BLOCK)
        parts = []
        for part in range(BLOCK // 128):
            there = pl.ds(pl.multiple_of(order[i * (BLOCK // 128) + part] * 128, 128), 128)
            parts.append(do_ref[there, :])
        back = jnp.concatenate(parts, axis=0).astype(bf16).astype(f32)
        first = lanes((BLOCK, 128)) < HEAD_SIZE
        product = back * attf_ref[here, :]
        delta0 = jnp.sum(jnp.where(first, product, 0.0), axis=1, keepdims=True)
        delta1 = jnp.sum(jnp.where(first, 0.0, product), axis=1, keepdims=True)
        delta = jnp.broadcast_to(jnp.concatenate([delta0, delta1], axis=0), (2 * BLOCK, 128))
        delta_ref[0, here, :] = delta[0:BLOCK]
        delta_ref[1, here, :] = delta[BLOCK : 2 * BLOCK]
        back0 = jnp.where(first, 0.0, pltpu.roll(back, HEAD_SIZE, 1)).astype(bf16)
        back1 = jnp.where(first, 0.0, back).astype(bf16)
        do2_ref[0, here, :] = back0
        do2_ref[1, here, :] = back1
        both = jnp.concatenate([back0, back1], axis=0)
        query = both_heads(q_ref, here)
        start = start_ref[here, :]
        lse = wide_lanes(both_heads(lse_ref, here))
        delta = wide_lanes(delta)

        def step(j, carry):
            base = pl.multiple_of(j * BLOCK, BLOCK)
            visible = seen(start, base - span, 0, False)
            back_query, back_kv = back_block(
                query, both, kvs[pl.ds(base, BLOCK), :], lse, delta, visible
            )
            dq_ref[0, here, :] += back_query[0:BLOCK]
            dq_ref[1, here, :] += back_query[BLOCK : 2 * BLOCK]
            dkvs[pl.ds(base, BLOCK), :] += back_kv
            return carry

        lax.fori_loop(first_block(low[i], span), span // BLOCK, step, 0)
    for n, ref in enumerate(outs):
        total = dkvs[pl.ds(n * count, count), :]
        ref[...] = (total * kv_scale(total.shape)).astype(bf16)


def back_own_kernel(
    low, start_ref, q_ref, kv_ref, do2_ref, delta_ref, lse_ref, dq_in_ref, dq_ref, dkv_ref
):
    count = q_ref.shape[1]
    dkv_ref[...] = jnp.zeros_like(dkv_ref)
    dq_ref[...] = dq_in_ref[...]
    for i in range(count // BLOCK):
        here = pl.ds(i * BLOCK, BLOCK)
        query = both_heads(q_ref, here)
        back = both_heads(do2_ref, here)
        start = start_ref[here, :]
        lse = wide_lanes(both_heads(lse_ref, here))
        delta = wide_lanes(both_heads(delta_ref, here))
        for j in range(i + 1):

            @pl.when(low[i] < (j + 1) * BLOCK)
            def _():
                visible = seen(start, j * BLOCK, i * BLOCK, j == i)
                keys = pl.ds(j * BLOCK, BLOCK)
                back_query, back_kv = back_block(
                    query, back, kv_ref[keys, :], lse, delta, visible
                )
                dq_ref[0, here, :] += back_query[0:BLOCK]
                dq_ref[1, here, :] += back_query[BLOCK : 2 * BLOCK]
                dkv_ref[keys, :] += back_kv

    total = dkv_ref[...]
    dkv_ref[...] = total * kv_scale(total.shape)


def rotary_back_kernel(
    order, pre_ref, cos_ref, sin_ref, qg_ref, kg_ref, dq_ref, dkv_ref, *rest
):
    received = rest[:-2]
    out_ref, gain_ref = rest[-2:]
    ones = block_ones()
    rows = 128
    gain_ref[...] = jnp.zeros_like(gain_ref)

    def step(j, carry):
        here = pl.ds(pl.multiple_of(j * rows, rows), rows)
        there = pl.ds(pl.multiple_of(order[j] * rows, rows), rows)
        cosine, sine = cos_ref[here, :], sin_ref[here, :]
        first = lanes((rows, 128)) < HEAD_SIZE

        def back(upstream, raw, gain):
            turned = upstream * cosine - swap_halves(upstream) * sine
            scaling = lax.rsqrt(head_mean(raw * raw, ones) + epsilon)
            normed = raw * scaling
            weighted = turned * gain
            inner = head_mean(weighted * normed, ones)
            return scaling * (weighted - normed * inner), turned * normed

        upstream = (
            jnp.where(first, dq_ref[0, here, :], pltpu.roll(dq_ref[1, here, :], HEAD_SIZE, 1))
            * score_scale
        )
        back_query, rows_query = back(upstream, pre_ref[there, 0:128], qg_ref[...])
        out_ref[there, 0:128] = back_query.astype(bf16)
        upstream = dkv_ref[here, :]
        for ref in received:
            upstream = upstream + ref[here, :].astype(f32)
        back_key, rows_key = back(upstream, pre_ref[there, 128:256], kg_ref[...])
        out_ref[there, 128:256] = jnp.where(first, back_key, upstream).astype(bf16)
        gain_ref[0:1, :] += jnp.sum(rows_query, axis=0, keepdims=True)
        gain_ref[1:2, :] += jnp.sum(jnp.where(first, rows_key, 0.0), axis=0, keepdims=True)
        return carry

    lax.fori_loop(0, pre_ref.shape[0] // rows, step, 0, unroll=2)


def half_tile(ref, index, place):
    tile = ref[:, (index // 2) * 128 : (index // 2 + 1) * 128].astype(f32)
    return tile if index % 2 == place else pltpu.roll(tile, HEAD_SIZE, 1)


def joined_halves(first, second):
    return jnp.where(lanes(first.shape) < HEAD_SIZE, first, second)


def pack_feed_kernel(g_ref, u_ref, d_ref, o_ref):
    share = g_ref.shape[1] // HEAD_SIZE // GROUP
    main = share // 2
    for m in range(GROUP):
        base = m * share
        for n, ref in enumerate((g_ref, u_ref)):
            for t in range(main):
                tile = joined_halves(
                    half_tile(ref, base + 2 * t, 0), half_tile(ref, base + 2 * t + 1, 1)
                )
                o_ref[m, :, (n * main + t) * 128 : (n * main + t + 1) * 128] = tile.astype(bf16)
        tile = joined_halves(
            half_tile(g_ref, base + share - 1, 0), half_tile(u_ref, base + share - 1, 1)
        )
        o_ref[m, :, 2 * main * 128 : (2 * main + 1) * 128] = tile.astype(bf16)
        begin = (2 * main + 1) * 128
        for t in range(main):
            tile = joined_halves(
                half_tile(d_ref, base + 2 * t, 0), half_tile(d_ref, base + 2 * t + 1, 1)
            )
            o_ref[m, :, begin + t * 128 : begin + (t + 1) * 128] = tile.astype(bf16)
        tile = half_tile(d_ref, base + share - 1, 0)
        o_ref[m, :, begin + main * 128 :] = tile[:, :HEAD_SIZE].astype(bf16)


def unpack_feed_kernel(i_ref, g_ref, u_ref, d_ref):
    share = g_ref.shape[1] // HEAD_SIZE // GROUP
    main = share // 2
    begin = (2 * main + 1) * 128

    def half(kind, index, place):
        m, h = index // share, index % share
        if kind == 2:
            if h == share - 1:
                part = i_ref[m, :, begin + main * 128 :].astype(f32)
                tile, side = jnp.concatenate([part, part], axis=1), place
            else:
                tile = i_ref[m, :, begin + (h // 2) * 128 : begin + (h // 2 + 1) * 128].astype(f32)
                side = h % 2
        elif h == share - 1:
            tile, side = i_ref[m, :, 2 * main * 128 : begin].astype(f32), kind
        else:
            at = kind * main + h // 2
            tile, side = i_ref[m, :, at * 128 : (at + 1) * 128].astype(f32), h % 2
        return tile if side == place else pltpu.roll(tile, HEAD_SIZE, 1)

    for kind, ref in enumerate((g_ref, u_ref, d_ref)):
        for t in range(ref.shape[1] // 128):
            ref[:, t * 128 : (t + 1) * 128] = joined_halves(
                half(kind, 2 * t, 0), half(kind, 2 * t + 1, 1)
            )


def pack_attention_kernel(q_ref, k_ref, v_ref, w_ref, o_ref):
    for m in range(GROUP):
        packed = jnp.concatenate(
            [
                q_ref[:, m * 128 : (m + 1) * 128],
                joined_halves(half_tile(k_ref, m, 0), half_tile(v_ref, m, 1)).astype(bf16),
                w_ref[:, m * 128 : (m + 1) * 128],
            ],
            axis=1,
        )
        for z in range(o_ref.shape[0] // GROUP):
            o_ref[z * GROUP + m] = packed


def unpack_attention_kernel(i_ref, q_ref, k_ref, v_ref, w_ref, gain_ref):
    rows = q_ref.shape[0]
    total = []
    for m in range(GROUP):
        part = i_ref[m, 0:rows, :].astype(f32)
        for z in range(1, i_ref.shape[0] // GROUP):
            part = part + i_ref[z * GROUP + m, 0:rows, :].astype(f32)
        total.append(part)
        q_ref[:, m * 128 : (m + 1) * 128] = part[:, 0:128]
        w_ref[:, m * 128 : (m + 1) * 128] = part[:, 256:384]
    for m in range(0, GROUP, 2):
        one, two = total[m][:, 128:256], total[m + 1][:, 128:256]
        at = slice(m * HEAD_SIZE, (m + 2) * HEAD_SIZE)
        k_ref[:, at] = joined_halves(one, pltpu.roll(two, HEAD_SIZE, 1))
        v_ref[:, at] = joined_halves(pltpu.roll(one, HEAD_SIZE, 1), two)
    gains = i_ref[0, rows:, :].astype(f32)
    for i in range(1, i_ref.shape[0]):
        gains = gains + i_ref[i, rows:, :].astype(f32)
    gain_ref[...] = gains[0 : gain_ref.shape[0]]


def join_kernel(*refs):
    rows = refs[0].shape[0]
    for i, ref in enumerate(refs[:-1]):
        refs[-1][i * rows : (i + 1) * rows, :] = ref[...]


def gather_rows(rows):
    parts = [rows] + [to_member(rows, flip) for flip in range(1, GROUP)]
    (own,) = call(
        join_kernel,
        [((GROUP * rows.shape[0], rows.shape[1]), rows.dtype)],
        [VMEM_WHOLE] * GROUP,
        name="join",
    )(*parts)
    return own, swap_core(own)


def product_kernel(a_ref, w_ref, o_ref):
    o_ref[...] = dot_t(a_ref[...], w_ref[...]).astype(o_ref.dtype)


def split_kernel(a_ref, w_ref, got_ref, own_ref, *parts):
    total = dot_t(a_ref[...], w_ref[...]) + got_ref[...].astype(f32)
    split_out(total, own_ref, parts)


def split_sum_kernel(mine_ref, got_ref, own_ref, *parts):
    split_out(mine_ref[...] + got_ref[...].astype(f32), own_ref, parts)


def split_out(total, own_ref, parts):
    rows = own_ref.shape[0]
    own_ref[...] = total[0:rows]
    for i, ref in enumerate(parts):
        ref[...] = total[(i + 1) * rows : (i + 2) * rows].astype(ref.dtype)


def spread(kernel, rows, width, operands, name):
    own, *parts = call(
        kernel,
        [((rows, width), f32)] + [((rows, width), bf16)] * (GROUP - 1),
        [VMEM_WHOLE] * len(operands),
        name=name,
    )(*operands)
    return [own] + [to_member(part, flip + 1) for flip, part in enumerate(parts)]


def product_rows(own, other, weight, name):
    width = weight.shape[0]
    (theirs,) = call(
        product_kernel, [((other.shape[0], width), bf16)], [VMEM_WHOLE] * 2, name=name + "_theirs"
    )(other, weight)
    rows = own.shape[0] // GROUP
    return spread(split_kernel, rows, width, (own, weight, swap_core(theirs)), name + "_mine")


def sum_of(refs):
    total = refs[0][...]
    for ref in refs[1:]:
        total = total + ref[...].astype(f32)
    return total


def hidden_kernel(*refs):
    terms, (x_ref, gain_ref, hidden_ref, feed_ref) = refs[:GROUP], refs[GROUP:]
    hidden = x_ref[...].astype(f32) + sum_of(terms)
    hidden_ref[...] = hidden
    feed_ref[...] = (hidden * rms_scale(hidden) * gain_ref[...]).astype(bf16)


def hidden_back_kernel(*refs):
    terms, rest = refs[:GROUP], refs[GROUP:]
    hidden_ref, gain_ref, dy_ref, back_ref, low_ref, part_ref = rest
    hidden, upstream = hidden_ref[...], sum_of(terms)
    back = dy_ref[...].astype(f32) + norm_back(upstream, hidden, gain_ref[...])
    back_ref[...] = back
    low_ref[...] = back.astype(bf16)
    part_ref[...] = jnp.sum(upstream * hidden * rms_scale(hidden), axis=0, keepdims=True)


def tokens_back_kernel(*refs):
    terms, (x_ref, gain_ref, back_ref, out_ref) = refs[:GROUP], refs[GROUP:]
    out_ref[...] = back_ref[...] + norm_back(sum_of(terms), x_ref[...].astype(f32), gain_ref[...])


def output_kernel(*refs):
    terms, (hidden_ref, out_ref) = refs[:GROUP], refs[GROUP:]
    out_ref[...] = (hidden_ref[...] + sum_of(terms)).astype(bf16)


def feed_kernel(x_ref, dy_ref, w_ref, back_ref, act_ref, both_ref):
    hidden_units = act_ref.shape[1]
    main = hidden_units // 128 * 128
    pair = 2 * hidden_units
    rows = 256

    def pieces(gate, up, back):
        sigmoid = 1.0 / (1.0 + jnp.exp(-gate))
        silu = gate * sigmoid
        slope = back * up * sigmoid * (1.0 + gate * (1.0 - sigmoid))
        return silu * up, slope, back * silu

    def step(i, carry):
        here = pl.ds(pl.multiple_of(i * rows, rows), rows)
        pre = jnp.dot(x_ref[here, :], w_ref[:, 0:pair], preferred_element_type=f32)
        back = jnp.dot(dy_ref[here, :], w_ref[:, pair:], preferred_element_type=f32)
        act, slope_gate, slope_up = pieces(
            pre[:, 0:main], pre[:, main : 2 * main], back[:, 0:main]
        )
        act_ref[here, 0:main] = act.astype(bf16)
        both_ref[here, 0:main] = slope_gate.astype(bf16)
        both_ref[here, main : 2 * main] = slope_up.astype(bf16)
        tail = pre[:, 2 * main : pair]
        back_tail = back[:, main:]
        back_tail = jnp.concatenate([back_tail, back_tail], axis=1)
        act, slope_gate, slope_up = pieces(tail, pltpu.roll(tail, HEAD_SIZE, 1), back_tail)
        act_ref[here, main:] = act[:, :HEAD_SIZE].astype(bf16)
        both_ref[here, 2 * main : pair] = joined_halves(
            slope_gate, pltpu.roll(slope_up, HEAD_SIZE, 1)
        ).astype(bf16)
        back_ref[here, :] = dot_t(both_ref[here, :], w_ref[:, 0:pair]).astype(back_ref.dtype)
        return carry

    lax.fori_loop(0, x_ref.shape[0] // rows, step, 0)


def slopes_kernel(xa_ref, xb_ref, ya_ref, yb_ref, ba_ref, bb_ref, aa_ref, ab_ref, o_ref):
    pair = ba_ref.shape[1]
    rows = 256

    def step(i, carry):
        here = pl.ds(pl.multiple_of(i * rows, rows), rows)
        one = dot_rows(xa_ref[:, here], ba_ref[...]) + dot_rows(xb_ref[:, here], bb_ref[...])
        o_ref[here, 0:pair] = one.astype(bf16)
        two = dot_rows(ya_ref[:, here], aa_ref[...]) + dot_rows(yb_ref[:, here], ab_ref[...])
        o_ref[here, pair:] = two.astype(bf16)
        return carry

    lax.fori_loop(0, o_ref.shape[0] // rows, step, 0)


def qkv_slope_kernel(xa_ref, xb_ref, b_ref, w_ref, gain_ref, o_ref, part_ref):
    half = xa_ref.shape[0]
    rows = 256
    ones = jnp.ones((8, b_ref.shape[1]), bf16)

    def step(i, carry):
        here = pl.ds(pl.multiple_of(i * rows, rows), rows)
        slope = dot_rows(xa_ref[:, here], b_ref[0:half, :])
        slope = slope + dot_rows(xb_ref[:, here], b_ref[half:, :])
        o_ref[here, :] = slope.astype(bf16)
        product = slope * w_ref[here, :].astype(f32)
        high = product.astype(bf16)
        low = (product - high.astype(f32)).astype(bf16)
        part_ref[:, here] = (dot_t(ones, high) + dot_t(ones, low)) / gain_ref[:, here]
        return carry

    lax.fori_loop(0, o_ref.shape[0] // rows, step, 0)


def output_slope_kernel(ra_ref, rb_ref, att_ref, o_ref):
    half = ra_ref.shape[0]
    rows = 256

    def step(i, carry):
        here = pl.ds(pl.multiple_of(i * rows, rows), rows)
        slope = dot_rows(ra_ref[:, here], att_ref[0:half, :])
        o_ref[here, :] = (slope + dot_rows(rb_ref[:, here], att_ref[half:, :])).astype(bf16)
        return carry

    lax.fori_loop(0, o_ref.shape[0] // rows, step, 0)


def on_device(
    tokens,
    positions,
    attention_gain,
    query_gain,
    key_gain,
    feedforward_gain,
    query_weight,
    key_matrix,
    value_matrix,
    output_weight,
    gate_weight,
    up_weight,
    down_weight,
    cotangent,
):
    size = lax.axis_size("ctx")
    outer = size // GROUP
    groups = [[GROUP * z + m for m in range(GROUP)] for z in range(outer)]
    columns = [[GROUP * z + m for z in range(outer)] for m in range(GROUP)]
    shard_rows, width = query_weight.shape[0], tokens.shape[1]
    own_rows = tokens.shape[0]
    count = 2 * GROUP * own_rows
    half = GROUP * own_rows
    units = gate_weight.shape[1] // GROUP
    halo_groups = -(-(DOC_MOST - 1) // count)
    member = lax.axis_index("ctx") % GROUP
    core = lax.axis_index("tp")
    attention_gains = attention_gain[None, :]
    feed_gains = feedforward_gain[None, :]

    (feed_pack,) = call(
        pack_feed_kernel, [((GROUP, shard_rows, 3 * units), bf16)], [VMEM_WHOLE] * 3, name="pack_feed"
    )(gate_weight, up_weight, down_weight)
    feed_pack = lax.all_to_all(feed_pack, "ctx", 0, 0, axis_index_groups=groups, tiled=True)
    feed_weight = lax.all_gather(
        feed_pack.reshape(GROUP * shard_rows, 3 * units),
        "ctx",
        axis=0,
        axis_index_groups=columns,
        tiled=True,
    )
    (attention_pack,) = call(
        pack_attention_kernel,
        [((size, shard_rows, 384), bf16)],
        [VMEM_WHOLE] * 4,
        name="pack_attention",
    )(query_weight, key_matrix, value_matrix, output_weight)
    attention_weights = lax.all_to_all(attention_pack, "ctx", 0, 0, tiled=True)
    attention_weights = attention_weights.reshape(width, 384)
    qkv_weight = attention_weights[:, :256]
    out_weight = attention_weights[:, 256:]

    residual = tokens.astype(f32)
    normed_rows = (residual * rms_scale(residual) * attention_gain).astype(bf16)
    entry_own, entry_other = gather_rows(normed_rows)

    block = jnp.arange(2 * GROUP, dtype=jnp.int32)
    order = ((block % 2) ^ core) * GROUP + ((block // 2) ^ member)
    place = positions.reshape(2, own_rows)
    near = jnp.stack([place] + [to_member(place, flip) for flip in range(1, GROUP)])
    near = near[jnp.arange(GROUP, dtype=jnp.int32) ^ member].reshape(count)
    start = jnp.arange(count, dtype=jnp.int32) - near
    low = start[::BLOCK]
    start_tile = jnp.broadcast_to(start[:, None], (count, 128))
    frequency = rope_base ** (
        -2.0 * jnp.arange(HEAD_SIZE // 2, dtype=f32) / HEAD_SIZE
    )
    angles = near.astype(f32)[:, None] * jnp.tile(frequency, 4)[None, :]
    cosine = jnp.cos(angles)
    sign = jnp.where(jnp.arange(128) % HEAD_SIZE < HEAD_SIZE // 2, -1.0, 1.0)
    sine = jnp.sin(angles) * sign[None, :]
    query_gains = jnp.tile(query_gain, 2)[None, :]
    key_gains = jnp.tile(key_gain, 2)[None, :]

    query, kv, pre = call(
        rotary_kernel,
        [((2, count, 128), bf16), ((count, 128), bf16), ((count, 256), f32)],
        [SMEM_WHOLE] + [VMEM_WHOLE] * 7,
        name="rotary",
    )(order, entry_own, entry_other, qkv_weight, cosine, sine, query_gains, key_gains)
    halo = [to_later(kv, GROUP * n) for n in range(halo_groups, 0, -1)]
    cotangent_in, _ = lax.optimization_barrier((cotangent, kv))
    dy_own, dy_other = gather_rows(cotangent_in)
    (own_part,) = call(
        attend_own_kernel,
        [((2, count, 128), f32)],
        [SMEM_WHOLE] + [VMEM_WHOLE] * 3,
        [pltpu.VMEM((2 * BLOCK, 128), f32)],
        name="attend_own",
    )(low, start_tile, query, kv)
    attended, attended_wide, lse = call(
        attend_halo_kernel,
        [((count, 128), bf16), ((count, 128), f32), ((2, count, 128), f32)],
        [SMEM_WHOLE] * 2 + [VMEM_WHOLE] * (3 + halo_groups),
        [pltpu.VMEM((halo_groups * count, 128), bf16), pltpu.VMEM((2 * BLOCK, 128), f32)],
        name="attend_halo",
    )(low, order, start_tile, query, own_part, *halo)
    terms = product_rows(attended[:half], attended[half:], out_weight, "attention_out")
    hidden, feed_rows = call(
        hidden_kernel,
        [((own_rows, width), f32), ((own_rows, width), bf16)],
        [VMEM_WHOLE] * (GROUP + 2),
        name="hidden",
    )(*terms, tokens, feed_gains)

    feed_own, feed_other = gather_rows(feed_rows)

    def feed(rows, dy, kind, name):
        return call(
            feed_kernel,
            [((half, width), kind), ((half, units), bf16), ((half, 2 * units), bf16)],
            [VMEM_WHOLE] * 3,
            name=name,
        )(rows, dy, feed_weight)

    theirs, act_other, both_other = feed(feed_other, dy_other, bf16, "feed_theirs")
    mine, act_own, both_own = feed(feed_own, dy_own, f32, "feed_mine")
    terms = spread(split_sum_kernel, own_rows, width, (mine, swap_core(theirs)), "feed_split")
    (feed_slope,) = call(
        slopes_kernel, [((width, 3 * units), bf16)], [VMEM_WHOLE] * 8, name="feed_slopes"
    )(feed_own, feed_other, dy_own, dy_other, both_own, both_other, act_own, act_other)
    back_hidden, back_low, feed_gain_part = call(
        hidden_back_kernel,
        [((own_rows, width), f32), ((own_rows, width), bf16), ((1, width), f32)],
        [VMEM_WHOLE] * (GROUP + 3),
        name="hidden_back",
    )(*terms, hidden, feed_gains, cotangent)
    residual_own, residual_other = gather_rows(back_low)

    feed_slope = lax.psum_scatter(
        feed_slope, "ctx", scatter_dimension=0, axis_index_groups=columns, tiled=True
    )
    feed_slope = lax.all_to_all(
        feed_slope.reshape(GROUP, shard_rows, 3 * units),
        "ctx",
        0,
        0,
        axis_index_groups=groups,
        tiled=True,
    )
    gate_out, up_out, down_out = call(
        unpack_feed_kernel, [((shard_rows, GROUP * units), f32)] * 3, [VMEM_WHOLE], name="unpack_feed"
    )(feed_slope)

    act_own, act_other, _ = lax.optimization_barrier((act_own, act_other, residual_other))
    terms = product_rows(act_own, act_other, feed_weight[:, 2 * units :], "down")
    (block_output,) = call(
        output_kernel, [((own_rows, width), bf16)], [VMEM_WHOLE] * (GROUP + 1), name="block_output"
    )(*terms, hidden)

    *back_halo, back_query_part, back_two, delta = call(
        back_halo_kernel,
        [((count, 128), bf16)] * halo_groups
        + [((2, count, 128), f32), ((2, count, 128), bf16), ((2, count, 128), f32)],
        [SMEM_WHOLE] * 2 + [VMEM_WHOLE] * (7 + halo_groups),
        [
            pltpu.VMEM((halo_groups * count, 128), bf16),
            pltpu.VMEM((halo_groups * count, 128), f32),
            pltpu.VMEM((count, 128), f32),
        ],
        name="back_halo",
    )(
        low,
        order,
        start_tile,
        query,
        residual_own,
        residual_other,
        out_weight,
        attended_wide,
        lse,
        *halo,
    )
    received = [
        to_later(part, -GROUP * n) for part, n in zip(back_halo, range(halo_groups, 0, -1))
    ]
    (output_slope,) = call(
        output_slope_kernel, [((width, 128), bf16)], [VMEM_WHOLE] * 3, name="output_slope"
    )(residual_own, residual_other, attended)
    back_query, back_kv = call(
        back_own_kernel,
        [((2, count, 128), f32), ((count, 128), f32)],
        [SMEM_WHOLE] + [VMEM_WHOLE] * 7,
        name="back_own",
    )(low, start_tile, query, kv, back_two, delta, lse, back_query_part)
    back_pre, head_gains = call(
        rotary_back_kernel,
        [((count, 256), bf16), ((8, 128), f32)],
        [SMEM_WHOLE] + [VMEM_WHOLE] * (7 + halo_groups),
        name="rotary_back",
    )(order, pre, cosine, sine, query_gains, key_gains, back_query, back_kv, *received)

    terms = product_rows(back_pre[:half], back_pre[half:], qkv_weight, "back_input")
    qkv_slope, attention_gain_part = call(
        qkv_slope_kernel, [((width, 256), bf16), ((8, width), f32)], [VMEM_WHOLE] * 5, name="qkv_slope"
    )(entry_own, entry_other, back_pre, qkv_weight, attention_gains)
    (dtokens,) = call(
        tokens_back_kernel, [((own_rows, width), f32)], [VMEM_WHOLE] * (GROUP + 3), name="tokens_back"
    )(*terms, tokens, attention_gains, back_hidden)

    gains = jnp.concatenate(
        [attention_gain_part[0], feed_gain_part[0], head_gains[0], head_gains[1]]
    )
    gains = jnp.pad(gains.reshape(-1, 384), ((0, 2), (0, 0))).astype(bf16)
    slope = jnp.concatenate([qkv_slope, output_slope], axis=1).reshape(size, shard_rows, 384)
    slope = jnp.concatenate([slope, jnp.broadcast_to(gains, (size, 8, 384))], axis=1)
    slope = lax.all_to_all(slope, "ctx", 0, 0, tiled=True)
    query_out, key_out, value_out, output_out, gains = call(
        unpack_attention_kernel,
        [
            ((shard_rows, 512), f32),
            ((shard_rows, 256), f32),
            ((shard_rows, 256), f32),
            ((shard_rows, 512), f32),
            ((8, 384), f32),
        ],
        [VMEM_WHOLE],
        name="unpack_attention",
    )(slope)
    gains = (gains + swap_core(gains)).reshape(-1)

    return (
        block_output,
        dtokens,
        gains[:width],
        gains[2 * width : 2 * width + 64] + gains[2 * width + 64 : 2 * width + 128],
        gains[2 * width + 128 : 2 * width + 192],
        gains[width : 2 * width],
        query_out,
        key_out,
        value_out,
        output_out,
        gate_out,
        up_out,
        down_out,
    )


def solution(mesh):
    rows = P(("ctx", "tp"), None)
    weight = P("ctx", "tp")
    return jax.shard_map(
        on_device,
        mesh=mesh,
        in_specs=(rows, P("ctx"), P(), P(), P(), P()) + (weight,) * 7 + (rows,),
        out_specs=(rows, rows, P(), P(), P(), P()) + (weight,) * 7,
        check_vma=False,
    )
```
